256 devices in a mesh: layer: 64 (over x, z, core), dp: 4 (over y).
Axes of the slice: x: 4, y: 4, z: 8, core: 2. Of those that a mesh axis runs over, the one named last changes fastest.
Arguments:
- cpoints: float32 [64, 4, 64, 1024], P('layer', 'dp'), parts along dimension 1, may hold values from -6 to 6
- network_input: float32 [4, 64, 1024], P('dp'), parts along dimension 0, may hold values from -6 to 6
- conv_weight: bfloat16 [3072, 64, 576], P('layer'), may hold values from -0.25 to 0.25
- conv_bias: float32 [3072, 64], P('layer'), may hold values from -3 to 3
- coarse_matrix: float32 [64, 64, 64], P('layer'), may hold values from -1 to 1
Outputs:
- block_final_states: float32 [64, 4, 64, 1024], P('layer', 'dp'), parts along dimension 1
- corrected: float32 [64, 4, 64, 1024], P('layer', 'dp'), parts along dimension 1
The draws below stay inside these ranges and needn't reach their ends.
There are 4 independent parts, one for each index of `dp`. The reference program is written for one: setup_inputs(seed, part) draws one part's arguments, and reference() takes and returns one part's arrays. A program takes and returns all parts, laid end to end along the dimension named above; an argument that names none is the same for every part. Nothing has to cross between parts.
All inputs are finite; a program needn't handle non-finite values.
Results may differ from the reference program's by a relative error of at most 0.0085.
Values sent between devices are 32-bit elements; how exact they have to be, the bound alone decides.
A program may use at most 64 MiB of HBM per device.

```python
import jax
import jax.numpy as jnp
from jax import lax

CH = 64
SIDE = 32
LAYERS_DEV = 48
IMGS = 1
SEGMENT_TOTAL = 64
LAYERS = 3072


def draw_coarse_matrix(key, part):
    sampler_seeds = jax.random.split(key, 8)
    twin_level_total = CH // 2
    slow_share = 0.5
    slow_decay = jax.random.uniform(sampler_seeds[0], (twin_level_total,)) < slow_share
    slow_rate = jnp.log(10.0) * jax.random.uniform(sampler_seeds[1], (twin_level_total,), minval=0.2, maxval=1.0) / SEGMENT_TOTAL
    fast_rate = jax.random.uniform(sampler_seeds[2], (twin_level_total,), minval=0.5, maxval=1.6)
    rates = jnp.where(slow_decay, slow_rate, fast_rate)
    wobble = jax.random.uniform(sampler_seeds[3], (SEGMENT_TOTAL, twin_level_total), minval=0.5, maxval=1.5)
    surviving_portion = jnp.exp(-rates[None, :] * wobble)
    segment_bundle = jax.random.uniform(sampler_seeds[4], (SEGMENT_TOTAL, twin_level_total)) < 3.0 / SEGMENT_TOTAL
    surviving_portion = surviving_portion * jnp.where(segment_bundle, jax.random.uniform(sampler_seeds[5], (SEGMENT_TOTAL, twin_level_total), minval=0.5, maxval=0.8), 1.0)
    turning = jax.random.uniform(sampler_seeds[6], (SEGMENT_TOTAL, twin_level_total), minval=0.2, maxval=0.45)
    turning = turning * jnp.where(jax.random.uniform(sampler_seeds[7], (SEGMENT_TOTAL, twin_level_total)) < 0.5, -1.0, 1.0)
    cosine = jnp.repeat(surviving_portion * jnp.cos(turning), 2, axis=1)
    sine = jnp.repeat(surviving_portion * jnp.sin(turning), 2, axis=1)
    channel = jnp.arange(CH)
    same_pair = channel[:, None] // 2 == channel[None, :] // 2
    diagonal = channel[:, None] == channel[None, :]
    orient = jnp.where(channel[:, None] % 2 == 0, -1.0, 1.0)
    matrix = jnp.where(diagonal[None], cosine[:, :, None], jnp.where(same_pair[None], orient[None] * sine[:, :, None], 0.0))
    return matrix.astype(jnp.float32)


def steps_of(stream_key, extent, shards, smallest, high):
    gain, own = 1.0, jax.random.fold_in(stream_key, 6)
    for position, blocks in shards:
        heights = jnp.exp(jax.random.uniform(jax.random.fold_in(own, position), (blocks,), jnp.float32, smallest / len(shards), high / len(shards)))
        gain = gain * jnp.repeat(heights, extent[position] // blocks).reshape([-1 if axis == position else 1 for axis in range(len(extent))])
    return gain


def scatter_about(stream_key, shape, deviation, limit, cuts=(), kind=jnp.bfloat16):
    result = jax.random.normal(stream_key, shape, jnp.float32) * deviation
    if len(cuts) > 0:
        result = steps_of(stream_key, shape, cuts, -0.22, 0.18) * result
    return jnp.clip(result, min=-limit, max=limit).astype(kind)


def setup_inputs(seed: int = 0, part: int = 0) -> dict:
    splits = jax.random.split(jax.random.key(seed), 6)
    own_keys = jax.random.split(jax.random.fold_in(splits[5], part), 6)
    cpoints = scatter_about(own_keys[0], (SEGMENT_TOTAL, IMGS, CH, SIDE * SIDE), 1.0, 6.0, ((0, 64),), jnp.float32)
    network_input = scatter_about(own_keys[1], (IMGS, CH, SIDE * SIDE), 1.0, 6.0, (), jnp.float32)
    conv_weight = scatter_about(splits[2], (LAYERS, CH, 9 * CH), (9 * CH) ** -0.5, 0.25, ((0, 64),))
    conv_bias = scatter_about(splits[3], (LAYERS, CH), 0.5, 3.0, ((0, 64),), jnp.float32)
    coarse_matrix = draw_coarse_matrix(jax.random.fold_in(splits[5], 71), part)
    return {"cpoints": cpoints, "network_input": network_input, "conv_weight": conv_weight, "conv_bias": conv_bias, "coarse_matrix": coarse_matrix}


step_size = 0.25


def unfold_taps(current):
    leading = current.shape[:-1]
    images = current.reshape(leading + (SIDE, SIDE))
    widths = [(0, 0)] * (images.ndim - 2) + [(1, 1), (1, 1)]
    padded = jnp.pad(images, widths)
    pieces = [padded[..., row_off:row_off + SIDE, col_off:col_off + SIDE].reshape(current.shape) for row_off in range(3) for col_off in range(3)]
    return jnp.concatenate(pieces, axis=-2)


def relax_all(starts, conv_weight, conv_bias):
    weights = conv_weight.reshape(SEGMENT_TOTAL, LAYERS_DEV, CH, 9 * CH).transpose(1, 0, 2, 3)
    biases = conv_bias.reshape(SEGMENT_TOTAL, LAYERS_DEV, CH).transpose(1, 0, 2)

    def advance(current, layer_pair):
        current_weight, bias_now = layer_pair
        stacked = unfold_taps(current.astype(jnp.bfloat16))
        mixed = jnp.einsum("koc,kicp->kiop", current_weight.astype(jnp.float32), stacked.astype(jnp.float32))
        return current + step_size * jnp.tanh(mixed + bias_now[:, None, :, None]), None

    final, unused = lax.scan(advance, starts, (weights, biases))
    return final


def reference(cpoints, network_input, conv_weight, conv_bias, coarse_matrix):
    ends = relax_all(cpoints, conv_weight, conv_bias)
    mismatch_vector = jnp.concatenate([(network_input - cpoints[0])[None], ends[:-1] - cpoints[1:]], axis=0)
    matrices = jnp.concatenate([jnp.zeros_like(coarse_matrix[:1]), coarse_matrix[:-1]], axis=0)

    def sweep(carried, pair):
        present_operator, residual_now = pair
        carried = jnp.einsum("cd,idp->icp", present_operator, carried, precision=lax.Precision.HIGHEST) + residual_now
        return carried, carried

    unused, correction = lax.scan(sweep, jnp.zeros_like(cpoints[0]), (matrices, mismatch_vector))
    corrected = cpoints + correction
    block_final_states = relax_all(corrected, conv_weight, conv_bias)
    return block_final_states, corrected
```

```python
import functools
import jax
import jax.numpy as jnp
from jax import lax
from jax.experimental import pallas as pl
from jax.experimental.pallas import tpu as pltpu
from jax.sharding import PartitionSpec as P

SIDE = 32
LANES = 128
step_size = 0.25


def to_bands(tiles):
    group = lax.broadcasted_iota(jnp.int32, tiles[0].shape, 1) // SIDE
    bands = []
    for band in range(8):
        out = None
        for slot in range(4):
            turn = SIDE * ((slot - band) % 4)
            tile = tiles[2 * slot + band // 4]
            tile = pltpu.roll(tile, turn, 1) if turn else tile
            out = tile if out is None else jnp.where(group == slot, tile, out)
        bands.append(out)
    return bands


def from_bands(bands):
    group = lax.broadcasted_iota(jnp.int32, bands[0].shape, 1) // SIDE
    tiles = []
    for tile in range(8):
        out = None
        for slot in range(4):
            turn = SIDE * ((slot - tile // 2) % 4)
            band = bands[4 * (tile % 2) + slot]
            band = pltpu.roll(band, turn, 1) if turn else band
            out = band if out is None else jnp.where(group == slot, band, out)
        tiles.append(out)
    return tiles


def split_lanes(value):
    return [value[:, LANES * k : LANES * (k + 1)] for k in range(value.shape[1] // LANES)]


def conv_layers(state_ref, weight_ref, bias_ref, unroll):
    ch = state_ref.shape[1]
    lane = lax.broadcasted_iota(jnp.int32, (ch, LANES), 1)
    column = lane % SIDE
    not_first, not_last = column != 0, column != SIDE - 1
    below, above = lane >= SIDE, lane < LANES - SIDE

    def layer(index, unused):
        weight = weight_ref[index]
        rows = jnp.concatenate([weight[:, 3 * ch * k : 3 * ch * (k + 1)] for k in range(3)], axis=0)
        bias = bias_ref[index]
        left, mid, right = [], [], []
        for band in range(8):
            value = state_ref[band]
            left.append(jnp.where(not_first, pltpu.roll(value, 1, 1), 0.0).astype(jnp.bfloat16))
            mid.append(value.astype(jnp.bfloat16))
            right.append(jnp.where(not_last, pltpu.roll(value, LANES - 1, 1), 0.0).astype(jnp.bfloat16))
        taps = []
        for pair in range(4):
            stack = jnp.concatenate(
                [jnp.concatenate(part[2 * pair : 2 * pair + 2], axis=1) for part in (left, mid, right)], axis=0
            )
            full = jnp.dot(rows, stack, preferred_element_type=jnp.float32)
            taps += [full[:, :LANES], full[:, LANES:]]
        for band in range(8):
            up = taps[band - 1][:ch]
            if band == 0:
                up = jnp.where(below, pltpu.roll(up, SIDE, 1), 0.0)
            down = taps[(band + 1) % 8][2 * ch :]
            if band == 7:
                down = jnp.where(above, pltpu.roll(down, LANES - SIDE, 1), 0.0)
            mixed = taps[band][ch : 2 * ch] + up + down
            state_ref[band] = state_ref[band] + step_size * jnp.tanh(mixed + bias)
        return unused

    lax.fori_loop(0, weight_ref.shape[0], layer, 0, unroll=unroll)


def block_kernel(start_ref, weight_ref, bias_ref, final_ref, state, unroll=1):
    for band, value in enumerate(to_bands(split_lanes(start_ref[...]))):
        state[band] = value
    conv_layers(state, weight_ref, bias_ref, unroll)
    for tile, value in enumerate(from_bands([state[band] for band in range(8)])):
        final_ref[:, LANES * tile : LANES * (tile + 1)] = value


def relax_block(start, conv_weight, bias_wide, unroll=1):
    ch, pixels = start.shape
    return pl.pallas_call(
        functools.partial(block_kernel, unroll=unroll),
        out_shape=jax.ShapeDtypeStruct((ch, pixels), jnp.float32),
        in_specs=[pl.BlockSpec(memory_space=pltpu.VMEM)] * 3,
        out_specs=pl.BlockSpec(memory_space=pltpu.VMEM),
        scratch_shapes=[pltpu.VMEM((8, ch, LANES), jnp.float32)],
        compiler_params=pltpu.CompilerParams(vmem_limit_bytes=60 << 20),
    )(start, conv_weight, bias_wide)


def from_behind(value, axis, steps):
    count = lax.axis_size(axis)
    initial, last = (max(0, -steps), min(count, count - steps))
    return lax.ppermute(value, axis, [(source, source + steps) for source in range(initial, last)])


def apply_matrix(matrix, field):
    return jnp.einsum("cd,idp->icp", matrix, field, precision=lax.Precision.HIGHEST)


def on_device(cpoints, network_input, conv_weight, conv_bias, coarse_matrix):
    start = cpoints[0]
    bias_wide = jnp.broadcast_to(conv_bias[:, :, None], conv_bias.shape + (LANES,))
    ends = relax_block(start[0], conv_weight, bias_wide)[None]
    received, matrix_in = from_behind((ends, coarse_matrix[0]), "layer", 1)
    leading_block = lax.axis_index("layer") == 0
    mismatch_vector = jnp.where(leading_block, network_input - start, received - start)

    def sweep_turn(counter, carried):
        previous = from_behind(carried, "layer", 1)
        return apply_matrix(matrix_in, previous) + mismatch_vector

    correction = lax.fori_loop(0, lax.axis_size("layer") - 1, sweep_turn, mismatch_vector)
    corrected = start + correction
    block_final_states = relax_block(corrected[0], conv_weight, bias_wide)[None]
    return (block_final_states[None], corrected[None])


def solution(mesh):
    placed = (
        P("layer", "dp", None, None),
        P("dp", None, None),
        P("layer", None, None),
        P("layer", None),
        P("layer", None, None),
    )
    return jax.shard_map(
        on_device,
        mesh=mesh,
        in_specs=placed,
        out_specs=(P("layer", "dp", None, None), P("layer", "dp", None, None)),
        check_vma=False,
    )
```

```python
import functools
import jax
import jax.numpy as jnp
from jax import lax
from jax.experimental import pallas as pl
from jax.experimental.pallas import tpu as pltpu
from jax.sharding import PartitionSpec as P

SIDE = 32
LANES = 128
step_size = 0.25


def to_bands(tiles):
    group = lax.broadcasted_iota(jnp.int32, tiles[0].shape, 1) // SIDE
    bands = []
    for band in range(8):
        out = None
        for slot in range(4):
            turn = SIDE * ((slot - band) % 4)
            tile = tiles[2 * slot + band // 4]
            tile = pltpu.roll(tile, turn, 1) if turn else tile
            out = tile if out is None else jnp.where(group == slot, tile, out)
        bands.append(out)
    return bands


def from_bands(bands):
    group = lax.broadcasted_iota(jnp.int32, bands[0].shape, 1) // SIDE
    tiles = []
    for tile in range(8):
        out = None
        for slot in range(4):
            turn = SIDE * ((slot - tile // 2) % 4)
            band = bands[4 * (tile % 2) + slot]
            band = pltpu.roll(band, turn, 1) if turn else band
            out = band if out is None else jnp.where(group == slot, band, out)
        tiles.append(out)
    return tiles


def split_lanes(value):
    return [value[:, LANES * k : LANES * (k + 1)] for k in range(value.shape[1] // LANES)]


def conv_layers(state_ref, weight_ref, bias_ref, first, last, unroll=1):
    ch = state_ref.shape[1]
    lane = lax.broadcasted_iota(jnp.int32, (ch, LANES), 1)
    column = lane % SIDE
    not_first, not_last = column != 0, column != SIDE - 1
    below, above = lane >= SIDE, lane < LANES - SIDE

    def layer(index, unused):
        weight = weight_ref[index]
        rows = jnp.concatenate([weight[:, 3 * ch * k : 3 * ch * (k + 1)] for k in range(3)], axis=0)
        bias = bias_ref[index]
        left, mid, right = [], [], []
        for band in range(8):
            value = state_ref[band]
            left.append(jnp.where(not_first, pltpu.roll(value, 1, 1), 0.0).astype(jnp.bfloat16))
            mid.append(value.astype(jnp.bfloat16))
            right.append(jnp.where(not_last, pltpu.roll(value, LANES - 1, 1), 0.0).astype(jnp.bfloat16))
        taps = []
        for pair in range(4):
            stack = jnp.concatenate(
                [jnp.concatenate(part[2 * pair : 2 * pair + 2], axis=1) for part in (left, mid, right)], axis=0
            )
            full = jnp.dot(rows, stack, preferred_element_type=jnp.float32)
            taps += [full[:, :LANES], full[:, LANES:]]
        for band in range(8):
            up = taps[band - 1][:ch]
            if band == 0:
                up = jnp.where(below, pltpu.roll(up, SIDE, 1), 0.0)
            down = taps[(band + 1) % 8][2 * ch :]
            if band == 7:
                down = jnp.where(above, pltpu.roll(down, LANES - SIDE, 1), 0.0)
            mixed = taps[band][ch : 2 * ch] + up + down
            state_ref[band] = state_ref[band] + step_size * jnp.tanh(mixed + bias)
        return unused

    lax.fori_loop(first, last, layer, 0, unroll=unroll)


def split_float(value):
    coarse = value.astype(jnp.bfloat16)
    return coarse, (value - coarse.astype(jnp.float32)).astype(jnp.bfloat16)


def cycle_kernel(
    count,
    start_ref,
    input_ref,
    weight_ref,
    bias_ref,
    matrix_ref,
    final_ref,
    corrected_ref,
    state,
    origin,
    matrix_t,
    start_t,
    ends_t,
    input_t,
    matrices,
    starts,
    ends,
    chain,
    returned,
    send_sems,
    recv_sems,
):
    me = lax.axis_index("layer")
    ch, pixels = start_ref.shape
    layers = weight_ref.shape[0]
    share = pixels // count
    early = layers // 4

    def slice_of(owner):
        return pl.ds(pl.multiple_of(owner * share, share), share)

    def push(source, target, number, peer):
        return pltpu.make_async_remote_copy(
            src_ref=source,
            dst_ref=target,
            send_sem=send_sems.at[number],
            recv_sem=recv_sems.at[number],
            device_id={"layer": peer},
            device_id_type=pl.DeviceIdType.MESH,
        )

    def peers(action):
        def turn(offset, unused):
            action(lax.rem(me + offset, count))
            return unused

        lax.fori_loop(1, count, turn, 0)

    def all_of(buffer, number):
        part = buffer.at[pl.ds(0, count - 1)]
        return push(part, part, number, lax.rem(me + 1, count))

    barrier = pltpu.get_barrier_semaphore()
    peers(
        lambda peer: pl.semaphore_signal(
            barrier, inc=1, device_id={"layer": peer}, device_id_type=pl.DeviceIdType.MESH
        )
    )
    matrix_t[...] = matrix_ref[...].T
    matrices[me] = matrix_ref[...].T
    for band, value in enumerate(to_bands(split_lanes(start_ref[...]))):
        state[band] = value
        origin[band] = value
        start_t[LANES * band : LANES * (band + 1), :] = value.T
    for band, value in enumerate(to_bands(split_lanes(input_ref[...]))):
        input_t[LANES * band : LANES * (band + 1), :] = value.T
    starts[me] = start_t[slice_of(me), :]
    conv_layers(state, weight_ref, bias_ref, 0, early)

    pl.semaphore_wait(barrier, count - 1)

    def send_early(peer):
        push(matrix_t, matrices.at[me], 0, peer).start()
        push(start_t.at[slice_of(peer)], starts.at[me], 1, peer).start()

    peers(send_early)
    conv_layers(state, weight_ref, bias_ref, early, layers)

    for band in range(8):
        ends_t[LANES * band : LANES * (band + 1), :] = state[band].T
    ends[me] = ends_t[slice_of(me), :]
    peers(lambda peer: push(ends_t.at[slice_of(peer)], ends.at[me], 2, peer).start())
    all_of(matrices, 0).wait_recv()
    all_of(starts, 1).wait_recv()
    all_of(ends, 2).wait_recv()

    def give(index):
        @pl.when(index != me)
        def _():
            push(chain.at[index], returned.at[me], 3, index).start()

    def chain_step(index, current):
        matrix_high, matrix_low = split_float(matrices[index - 1])
        high, low = split_float(current)
        both = jnp.dot(
            jnp.concatenate([high, low], axis=0), matrix_high, preferred_element_type=jnp.float32
        )
        rest = jnp.dot(high, matrix_low, preferred_element_type=jnp.float32)
        current = both[:share] + both[share:] + rest + (ends[index - 1] - starts[index])
        chain[index] = current
        give(index - 1)
        return current

    first = input_t[slice_of(me), :] - starts[0]
    chain[0] = first
    lax.fori_loop(1, count, chain_step, first, unroll=3)
    give(count - 1)
    returned[me] = chain[me]
    all_of(returned, 3).wait_recv()

    corrected = []
    gathered = returned[...].reshape(pixels, ch)
    for band in range(8):
        part = gathered[LANES * band : LANES * (band + 1)]
        corrected.append(origin[band] + part.T)
        state[band] = corrected[band]
    for tile, value in enumerate(from_bands(corrected)):
        corrected_ref[:, LANES * tile : LANES * (tile + 1)] = value
    conv_layers(state, weight_ref, bias_ref, 0, layers)
    for tile, value in enumerate(from_bands([state[band] for band in range(8)])):
        final_ref[:, LANES * tile : LANES * (tile + 1)] = value
    for number, buffer in enumerate((matrices, starts, ends, returned)):
        all_of(buffer, number).wait_send()


def on_device(cpoints, network_input, conv_weight, conv_bias, coarse_matrix):
    ch, pixels = network_input.shape[1:]
    count = lax.axis_size("layer")
    share = pixels // count
    bias_wide = jnp.broadcast_to(conv_bias[:, :, None], conv_bias.shape + (LANES,))
    state = jax.ShapeDtypeStruct((ch, pixels), jnp.float32)
    transposed = pltpu.VMEM((pixels, ch), jnp.float32)
    gathered = pltpu.VMEM((count, share, ch), jnp.float32)
    final, corrected = pl.pallas_call(
        functools.partial(cycle_kernel, count),
        out_shape=(state, state),
        in_specs=[pl.BlockSpec(memory_space=pltpu.VMEM)] * 5,
        out_specs=(pl.BlockSpec(memory_space=pltpu.VMEM),) * 2,
        scratch_shapes=[
            pltpu.VMEM((8, ch, LANES), jnp.float32),
            pltpu.VMEM((8, ch, LANES), jnp.float32),
            pltpu.VMEM((ch, ch), jnp.float32),
            transposed,
            transposed,
            transposed,
            pltpu.VMEM((count, ch, ch), jnp.float32),
            gathered,
            gathered,
            gathered,
            gathered,
            pltpu.SemaphoreType.DMA((4,)),
            pltpu.SemaphoreType.DMA((4,)),
        ],
        compiler_params=pltpu.CompilerParams(
            collective_id=0, has_side_effects=True, vmem_limit_bytes=60 << 20
        ),
    )(cpoints[0, 0], network_input[0], conv_weight, bias_wide, coarse_matrix[0])
    return (final[None, None], corrected[None, None])


def solution(mesh):
    placed = (
        P("layer", "dp", None, None),
        P("dp", None, None),
        P("layer", None, None),
        P("layer", None),
        P("layer", None, None),
    )
    return jax.shard_map(
        on_device,
        mesh=mesh,
        in_specs=placed,
        out_specs=(P("layer", "dp", None, None), P("layer", "dp", None, None)),
        check_vma=False,
    )
```

```python
import functools
import jax
import jax.numpy as jnp
from jax import lax
from jax.experimental import pallas as pl
from jax.experimental.pallas import tpu as pltpu
from jax.sharding import PartitionSpec as P

SIDE = 32
LANES = 128
step_size = 0.25


def to_bands(tiles):
    group = lax.broadcasted_iota(jnp.int32, tiles[0].shape, 1) // SIDE
    bands = []
    for band in range(8):
        out = None
        for slot in range(4):
            turn = SIDE * ((slot - band) % 4)
            tile = tiles[2 * slot + band // 4]
            tile = pltpu.roll(tile, turn, 1) if turn else tile
            out = tile if out is None else jnp.where(group == slot, tile, out)
        bands.append(out)
    return bands


def from_bands(bands):
    group = lax.broadcasted_iota(jnp.int32, bands[0].shape, 1) // SIDE
    tiles = []
    for tile in range(8):
        out = None
        for slot in range(4):
            turn = SIDE * ((slot - tile // 2) % 4)
            band = bands[4 * (tile % 2) + slot]
            band = pltpu.roll(band, turn, 1) if turn else band
            out = band if out is None else jnp.where(group == slot, band, out)
        tiles.append(out)
    return tiles


def split_lanes(value):
    return [value[:, LANES * k : LANES * (k + 1)] for k in range(value.shape[1] // LANES)]


def conv_layers(state_ref, weight_ref, bias_ref, first, last, unroll=1):
    ch = state_ref.shape[1]
    lane = lax.broadcasted_iota(jnp.int32, (ch, LANES), 1)
    column = lane % SIDE
    not_first, not_last = column != 0, column != SIDE - 1
    below, above = lane >= SIDE, lane < LANES - SIDE

    def layer(index, unused):
        weight = weight_ref[index]
        rows = jnp.concatenate([weight[:, 3 * ch * k : 3 * ch * (k + 1)] for k in range(3)], axis=0)
        bias = bias_ref[index]
        left, mid, right = [], [], []
        for band in range(8):
            value = state_ref[band]
            left.append(jnp.where(not_first, pltpu.roll(value, 1, 1), 0.0).astype(jnp.bfloat16))
            mid.append(value.astype(jnp.bfloat16))
            right.append(jnp.where(not_last, pltpu.roll(value, LANES - 1, 1), 0.0).astype(jnp.bfloat16))
        taps = []
        for pair in range(4):
            stack = jnp.concatenate(
                [jnp.concatenate(part[2 * pair : 2 * pair + 2], axis=1) for part in (left, mid, right)], axis=0
            )
            full = jnp.dot(rows, stack, preferred_element_type=jnp.float32)
            taps += [full[:, :LANES], full[:, LANES:]]
        for band in range(8):
            up = taps[band - 1][:ch]
            if band == 0:
                up = jnp.where(below, pltpu.roll(up, SIDE, 1), 0.0)
            down = taps[(band + 1) % 8][2 * ch :]
            if band == 7:
                down = jnp.where(above, pltpu.roll(down, LANES - SIDE, 1), 0.0)
            mixed = taps[band][ch : 2 * ch] + up + down
            state_ref[band] = state_ref[band] + step_size * jnp.tanh(mixed + bias)
        return unused

    lax.fori_loop(first, last, layer, 0, unroll=unroll)


def split_float(value):
    coarse = value.astype(jnp.bfloat16)
    return coarse, (value - coarse.astype(jnp.float32)).astype(jnp.bfloat16)


def cycle_kernel(
    count,
    start_ref,
    input_ref,
    weight_hbm,
    bias_ref,
    matrix_ref,
    final_ref,
    corrected_ref,
    weights,
    biases,
    state,
    origin,
    starts_out,
    ends_out,
    input_out,
    matrices,
    coarse_high,
    coarse_low,
    starts,
    ends,
    chain,
    returned,
    load_sems,
    send_sems,
    recv_sems,
):
    me = lax.axis_index("layer")
    core = lax.rem(me, 2)
    chips = count // 2
    ch, pixels = start_ref.shape
    layers = weights.shape[0]
    share = pixels // 2 // count
    early, late = layers // 6, 2 * layers // 3

    loads = [
        pltpu.make_async_copy(weight_hbm.at[part], weights.at[part], load_sems.at[number])
        for number, part in enumerate((pl.ds(0, early), pl.ds(early, layers - early)))
    ]
    for load in loads:
        load.start()

    def slice_of(owner):
        return pl.ds(pl.multiple_of(owner * share, share), share)

    def push(source, target, number, peer):
        return pltpu.make_async_remote_copy(
            src_ref=source,
            dst_ref=target,
            send_sem=send_sems.at[number],
            recv_sem=recv_sems.at[number],
            device_id={"layer": peer},
            device_id_type=pl.DeviceIdType.MESH,
        )

    def peers(action, stride=1):
        def turn(offset, unused):
            action(lax.rem(me + offset * stride, count))
            return unused

        lax.fori_loop(1, count // stride, turn, 0)

    def all_of(buffer, number):
        return push(buffer, buffer, number, lax.rem(me + 1, count))

    def packed(bands):
        return [jnp.concatenate([bands[k], bands[k + 4]], axis=0).T for k in range(4)]

    barrier = pltpu.get_barrier_semaphore()
    peers(
        lambda peer: pl.semaphore_signal(
            barrier, inc=1, device_id={"layer": peer}, device_id_type=pl.DeviceIdType.MESH
        )
    )
    turned = matrix_ref[...].T
    matrices[core, me // 2] = jnp.concatenate([turned[: ch // 2], turned[ch // 2 :]], axis=1)
    columns = bias_ref[...].T
    for index in range(layers):
        biases[index] = jnp.broadcast_to(columns[:, index : index + 1], (ch, LANES))
    bands = to_bands(split_lanes(start_ref[...]))
    for band in range(8):
        state[band] = bands[band]
        origin[band] = bands[band]
    for part, value in enumerate(packed(bands)):
        starts_out[LANES * part : LANES * (part + 1), :] = value
    for part, value in enumerate(packed(to_bands(split_lanes(input_ref[...])))):
        input_out[LANES * part : LANES * (part + 1), :] = value
    starts[me] = starts_out[slice_of(me), :]
    loads[0].wait()
    conv_layers(state, weights, biases, 0, early)

    pl.semaphore_wait(barrier, count - 1)
    own = matrices.at[core, me // 2]
    peers(lambda peer: push(own, own, 0, peer).start(), 2)
    peers(lambda peer: push(starts_out.at[slice_of(peer)], starts.at[me], 1, peer).start())
    loads[1].wait()
    conv_layers(state, weights, biases, early, late)

    all_of(matrices.at[0, pl.ds(0, chips - 1)], 0).wait_recv()
    across = push(matrices.at[core], matrices.at[core], 4, me + 1 - 2 * core)
    across.start()
    conv_layers(state, weights, biases, late, layers)

    for part, value in enumerate(packed([state[band] for band in range(8)])):
        ends_out[LANES * part : LANES * (part + 1), :] = value
    ends[me] = ends_out[slice_of(me), :]
    peers(lambda peer: push(ends_out.at[slice_of(peer)], ends.at[me], 2, peer).start())
    across.wait_recv()
    lower = lax.broadcasted_iota(jnp.int32, (ch // 2, LANES), 1) < ch

    def widen(index, unused):
        pair = matrices[lax.rem(index, 2), index // 2]
        swapped = pltpu.roll(pair, ch, 1)
        wide = jnp.concatenate(
            [
                jnp.where(lower, pair, 0.0),
                jnp.where(lower, swapped, 0.0),
                jnp.where(lower, 0.0, swapped),
                jnp.where(lower, 0.0, pair),
            ],
            axis=0,
        )
        high, low = split_float(wide)
        coarse_high[index] = high
        coarse_low[index] = low
        return unused

    lax.fori_loop(0, count - 1, widen, 0)
    all_of(starts.at[pl.ds(0, count - 1)], 1).wait_recv()
    all_of(ends.at[pl.ds(0, count - 1)], 2).wait_recv()

    def give(index):
        @pl.when(index != me)
        def _():
            push(chain.at[index], returned.at[me], 3, index).start()

    def chain_step(index, current):
        matrix_high, matrix_low = coarse_high[index - 1], coarse_low[index - 1]
        high, low = split_float(current)
        both = jnp.dot(
            jnp.concatenate([high, low], axis=0), matrix_high, preferred_element_type=jnp.float32
        )
        rest = jnp.dot(high, matrix_low, preferred_element_type=jnp.float32)
        current = both[:share] + both[share:] + rest + (ends[index - 1] - starts[index])
        chain[index] = current
        give(index - 1)
        return current

    first = input_out[slice_of(me), :] - starts[0]
    chain[0] = first
    lax.fori_loop(1, count, chain_step, first, unroll=3)
    give(count - 1)
    returned[me] = chain[me]
    all_of(returned.at[pl.ds(0, count - 1)], 3).wait_recv()

    gathered = returned[...].reshape(pixels // 2, LANES)
    corrected = [None] * 8
    for part in range(4):
        both = gathered[LANES * part : LANES * (part + 1)].T
        corrected[part] = origin[part] + both[:ch]
        corrected[part + 4] = origin[part + 4] + both[ch:]
    for band in range(8):
        state[band] = corrected[band]
    for tile, value in enumerate(from_bands(corrected)):
        corrected_ref[:, LANES * tile : LANES * (tile + 1)] = value
    conv_layers(state, weights, biases, 0, layers)
    for tile, value in enumerate(from_bands([state[band] for band in range(8)])):
        final_ref[:, LANES * tile : LANES * (tile + 1)] = value
    all_of(matrices.at[0, pl.ds(0, chips - 1)], 0).wait_send()
    across.wait_send()
    for number, buffer in ((1, starts), (2, ends), (3, returned)):
        all_of(buffer.at[pl.ds(0, count - 1)], number).wait_send()


def on_device(cpoints, network_input, conv_weight, conv_bias, coarse_matrix):
    ch, pixels = network_input.shape[1:]
    layers = conv_bias.shape[0]
    count = lax.axis_size("layer")
    share = pixels // 2 // count
    state = jax.ShapeDtypeStruct((ch, pixels), jnp.float32)
    banded = pltpu.VMEM((8, ch, LANES), jnp.float32)
    sent = pltpu.VMEM((pixels // 2, LANES), jnp.float32)
    gathered = pltpu.VMEM((count, share, LANES), jnp.float32)
    wide = pltpu.VMEM((count, LANES, LANES), jnp.bfloat16)
    vmem = pl.BlockSpec(memory_space=pltpu.VMEM)
    final, corrected = pl.pallas_call(
        functools.partial(cycle_kernel, count),
        out_shape=(state, state),
        in_specs=[vmem, vmem, pl.BlockSpec(memory_space=pl.ANY), vmem, vmem],
        out_specs=(vmem, vmem),
        scratch_shapes=[
            pltpu.VMEM(conv_weight.shape, conv_weight.dtype),
            pltpu.VMEM((layers, ch, LANES), jnp.float32),
            banded,
            banded,
            sent,
            sent,
            sent,
            pltpu.VMEM((2, count // 2, ch // 2, LANES), jnp.float32),
            wide,
            wide,
            gathered,
            gathered,
            gathered,
            gathered,
            pltpu.SemaphoreType.DMA((2,)),
            pltpu.SemaphoreType.DMA((5,)),
            pltpu.SemaphoreType.DMA((5,)),
        ],
        compiler_params=pltpu.CompilerParams(
            collective_id=0, has_side_effects=True, vmem_limit_bytes=60 << 20
        ),
    )(cpoints[0, 0], network_input[0], conv_weight, conv_bias, coarse_matrix[0])
    return (final[None, None], corrected[None, None])


def solution(mesh):
    placed = (
        P("layer", "dp", None, None),
        P("dp", None, None),
        P("layer", None, None),
        P("layer", None),
        P("layer", None, None),
    )
    return jax.shard_map(
        on_device,
        mesh=mesh,
        in_specs=placed,
        out_specs=(P("layer", "dp", None, None), P("layer", "dp", None, None)),
        check_vma=False,
    )
```

```python
import functools
import jax
import jax.numpy as jnp
from jax import lax
from jax.experimental import pallas as pl
from jax.experimental.pallas import tpu as pltpu
from jax.sharding import PartitionSpec as P

SIDE = 32
LANES = 128
step_size = 0.25


def to_bands(tiles):
    group = lax.broadcasted_iota(jnp.int32, tiles[0].shape, 1) // SIDE
    bands = []
    for band in range(8):
        out = None
        for slot in range(4):
            turn = SIDE * ((slot - band) % 4)
            tile = tiles[2 * slot + band // 4]
            tile = pltpu.roll(tile, turn, 1) if turn else tile
            out = tile if out is None else jnp.where(group == slot, tile, out)
        bands.append(out)
    return bands


def from_bands(bands):
    group = lax.broadcasted_iota(jnp.int32, bands[0].shape, 1) // SIDE
    tiles = []
    for tile in range(8):
        out = None
        for slot in range(4):
            turn = SIDE * ((slot - tile // 2) % 4)
            band = bands[4 * (tile % 2) + slot]
            band = pltpu.roll(band, turn, 1) if turn else band
            out = band if out is None else jnp.where(group == slot, band, out)
        tiles.append(out)
    return tiles


def split_lanes(value):
    return [value[:, LANES * k : LANES * (k + 1)] for k in range(value.shape[1] // LANES)]


def conv_layers(state_ref, weight_ref, bias_ref, first, last, unroll):
    ch = state_ref.shape[1]
    lane = lax.broadcasted_iota(jnp.int32, (ch, LANES), 1)
    column = lane % SIDE
    not_first, not_last = column != 0, column != SIDE - 1
    below, above = lane >= SIDE, lane < LANES - SIDE

    def layer(index, unused):
        weight = weight_ref[index]
        rows = jnp.concatenate([weight[:, 3 * ch * k : 3 * ch * (k + 1)] for k in range(3)], axis=0)
        bias = bias_ref[index]
        left, mid, right = [], [], []
        for band in range(8):
            value = state_ref[band]
            value = value.astype(jnp.bfloat16)
            zero = jnp.zeros_like(value)
            left.append(jnp.where(not_first, pltpu.roll(value, 1, 1), zero))
            mid.append(value)
            right.append(jnp.where(not_last, pltpu.roll(value, LANES - 1, 1), zero))
        taps = []
        for pair in range(4):
            stack = jnp.concatenate(
                [jnp.concatenate(part[2 * pair : 2 * pair + 2], axis=1) for part in (left, mid, right)], axis=0
            )
            full = jnp.dot(rows, stack, preferred_element_type=jnp.float32)
            taps += [full[:, :LANES], full[:, LANES:]]
        for band in range(8):
            up = taps[band - 1][:ch]
            if band == 0:
                up = jnp.where(below, pltpu.roll(up, SIDE, 1), 0.0)
            down = taps[(band + 1) % 8][2 * ch :]
            if band == 7:
                down = jnp.where(above, pltpu.roll(down, LANES - SIDE, 1), 0.0)
            mixed = taps[band][ch : 2 * ch] + up + down
            state_ref[band] = state_ref[band] + step_size * jnp.tanh(mixed + bias)
        return unused

    lax.fori_loop(first, last, layer, 0, unroll=unroll)


def split_float(value):
    coarse = value.astype(jnp.bfloat16)
    return coarse, (value - coarse.astype(jnp.float32)).astype(jnp.bfloat16)


def cycle_kernel(
    count,
    start_ref,
    input_ref,
    weight_hbm,
    bias_ref,
    matrix_ref,
    final_ref,
    corrected_ref,
    weights,
    biases,
    state,
    origin,
    starts_out,
    ends_out,
    input_out,
    matrices,
    coarse_high,
    coarse_low,
    starts,
    ends,
    chain,
    returned,
    load_sems,
    send_sems,
    recv_sems,
):
    me = lax.axis_index("layer")
    core = lax.rem(me, 2)
    chips = count // 2
    ch, pixels = start_ref.shape
    layers = weights.shape[0]
    share = pixels // 2 // count
    early, late = layers // 6, 2 * layers // 3
    unroll = 4 if early % 4 == 0 else 1

    loads = [
        pltpu.make_async_copy(weight_hbm.at[part], weights.at[part], load_sems.at[number])
        for number, part in enumerate((pl.ds(0, early), pl.ds(early, layers - early)))
    ]
    for load in loads:
        load.start()

    def slice_of(owner):
        return pl.ds(pl.multiple_of(owner * share, share), share)

    def push(source, target, number, peer):
        return pltpu.make_async_remote_copy(
            src_ref=source,
            dst_ref=target,
            send_sem=send_sems.at[number],
            recv_sem=recv_sems.at[number],
            device_id={"layer": peer},
            device_id_type=pl.DeviceIdType.MESH,
        )

    def peers(action, stride=1):
        def turn(offset, unused):
            action(lax.rem(me + offset * stride, count))
            return unused

        lax.fori_loop(1, count // stride, turn, 0, unroll=3 if stride == 1 else 1)

    def all_of(buffer, number):
        return push(buffer, buffer, number, lax.rem(me + 1, count))

    def packed(bands):
        return [jnp.concatenate([bands[k], bands[k + 4]], axis=0).T for k in range(4)]

    barrier = pltpu.get_barrier_semaphore()
    peers(
        lambda peer: pl.semaphore_signal(
            barrier, inc=1, device_id={"layer": peer}, device_id_type=pl.DeviceIdType.MESH
        )
    )
    turned = matrix_ref[...].T
    matrices[core, me // 2] = jnp.concatenate([turned[: ch // 2], turned[ch // 2 :]], axis=1)
    columns = bias_ref[...].T
    for index in range(layers):
        biases[index] = jnp.broadcast_to(columns[:, index : index + 1], (ch, LANES))
    bands = to_bands(split_lanes(start_ref[...]))
    for band in range(8):
        state[band] = bands[band]
        origin[band] = bands[band]
    for part, value in enumerate(packed(bands)):
        starts_out[LANES * part : LANES * (part + 1), :] = value
    starts[me] = starts_out[slice_of(me), :]
    loads[0].wait()
    conv_layers(state, weights, biases, 0, early, unroll)

    pl.semaphore_wait(barrier, count - 1)
    own = matrices.at[core, me // 2]
    peers(lambda peer: push(own, own, 0, peer).start(), 2)
    peers(lambda peer: push(starts_out.at[slice_of(peer)], starts.at[me], 1, peer).start())
    loads[1].wait()
    conv_layers(state, weights, biases, early, late, unroll)

    all_of(matrices.at[0, pl.ds(0, chips - 1)], 0).wait_recv()
    across = push(matrices.at[core], matrices.at[core], 4, me + 1 - 2 * core)
    across.start()
    conv_layers(state, weights, biases, late, layers, unroll)

    for part, value in enumerate(packed([state[band] for band in range(8)])):
        ends_out[LANES * part : LANES * (part + 1), :] = value
    ends[me] = ends_out[slice_of(me), :]
    peers(lambda peer: push(ends_out.at[slice_of(peer)], ends.at[me], 2, peer).start())
    for part, value in enumerate(packed(to_bands(split_lanes(input_ref[...])))):
        input_out[LANES * part : LANES * (part + 1), :] = value
    across.wait_recv()
    lower = lax.broadcasted_iota(jnp.int32, (ch // 2, LANES), 1) < ch

    def widen(index, unused):
        pair = matrices[lax.rem(index, 2), index // 2]
        swapped = pltpu.roll(pair, ch, 1)
        wide = jnp.concatenate(
            [
                jnp.where(lower, pair, 0.0),
                jnp.where(lower, swapped, 0.0),
                jnp.where(lower, 0.0, swapped),
                jnp.where(lower, 0.0, pair),
            ],
            axis=0,
        )
        high, low = split_float(wide)
        coarse_high[index] = high
        coarse_low[index] = low
        return unused

    lax.fori_loop(0, count - 1, widen, 0, unroll=3)
    all_of(starts.at[pl.ds(0, count - 1)], 1).wait_recv()
    all_of(ends.at[pl.ds(0, count - 1)], 2).wait_recv()

    def give(index):
        @pl.when(index != me)
        def _():
            push(chain.at[index], returned.at[me], 3, index).start()

    def chain_step(index, current):
        matrix_high, matrix_low = coarse_high[index - 1], coarse_low[index - 1]
        high, low = split_float(current)
        both = jnp.dot(
            jnp.concatenate([high, low], axis=0), matrix_high, preferred_element_type=jnp.float32
        )
        rest = jnp.dot(high, matrix_low, preferred_element_type=jnp.float32)
        current = both[:share] + both[share:] + rest + (ends[index - 1] - starts[index])
        chain[index] = current
        give(index - 1)
        return current

    first = input_out[slice_of(me), :] - starts[0]
    chain[0] = first
    lax.fori_loop(1, count, chain_step, first, unroll=3)
    give(count - 1)
    returned[me] = chain[me]
    all_of(returned.at[pl.ds(0, count - 1)], 3).wait_recv()

    gathered = returned[...].reshape(pixels // 2, LANES)
    corrected = [None] * 8
    for part in range(4):
        both = gathered[LANES * part : LANES * (part + 1)].T
        corrected[part] = origin[part] + both[:ch]
        corrected[part + 4] = origin[part + 4] + both[ch:]
    for band in range(8):
        state[band] = corrected[band]
    for tile, value in enumerate(from_bands(corrected)):
        corrected_ref[:, LANES * tile : LANES * (tile + 1)] = value
    conv_layers(state, weights, biases, 0, layers, unroll)
    for tile, value in enumerate(from_bands([state[band] for band in range(8)])):
        final_ref[:, LANES * tile : LANES * (tile + 1)] = value
    all_of(matrices.at[0, pl.ds(0, chips - 1)], 0).wait_send()
    across.wait_send()
    for number, buffer in ((1, starts), (2, ends), (3, returned)):
        all_of(buffer.at[pl.ds(0, count - 1)], number).wait_send()


def on_device(cpoints, network_input, conv_weight, conv_bias, coarse_matrix):
    ch, pixels = network_input.shape[1:]
    layers = conv_bias.shape[0]
    count = lax.axis_size("layer")
    share = pixels // 2 // count
    state = jax.ShapeDtypeStruct((ch, pixels), jnp.float32)
    banded = pltpu.VMEM((8, ch, LANES), jnp.float32)
    sent = pltpu.VMEM((pixels // 2, LANES), jnp.float32)
    gathered = pltpu.VMEM((count, share, LANES), jnp.float32)
    wide = pltpu.VMEM((count, LANES, LANES), jnp.bfloat16)
    vmem = pl.BlockSpec(memory_space=pltpu.VMEM)
    final, corrected = pl.pallas_call(
        functools.partial(cycle_kernel, count),
        out_shape=(state, state),
        in_specs=[vmem, vmem, pl.BlockSpec(memory_space=pl.ANY), vmem, vmem],
        out_specs=(vmem, vmem),
        scratch_shapes=[
            pltpu.VMEM(conv_weight.shape, conv_weight.dtype),
            pltpu.VMEM((layers, ch, LANES), jnp.float32),
            banded,
            banded,
            sent,
            sent,
            sent,
            pltpu.VMEM((2, count // 2, ch // 2, LANES), jnp.float32),
            wide,
            wide,
            gathered,
            gathered,
            gathered,
            gathered,
            pltpu.SemaphoreType.DMA((2,)),
            pltpu.SemaphoreType.DMA((5,)),
            pltpu.SemaphoreType.DMA((5,)),
        ],
        compiler_params=pltpu.CompilerParams(
            collective_id=0, has_side_effects=True, vmem_limit_bytes=60 << 20
        ),
    )(cpoints[0, 0], network_input[0], conv_weight, conv_bias, coarse_matrix[0])
    return (final[None, None], corrected[None, None])


def solution(mesh):
    placed = (
        P("layer", "dp", None, None),
        P("dp", None, None),
        P("layer", None, None),
        P("layer", None),
        P("layer", None, None),
    )
    return jax.shard_map(
        on_device,
        mesh=mesh,
        in_specs=placed,
        out_specs=(P("layer", "dp", None, None), P("layer", "dp", None, None)),
        check_vma=False,
    )
```

```python
import functools
import jax
import jax.numpy as jnp
from jax import lax
from jax.experimental import pallas as pl
from jax.experimental.pallas import tpu as pltpu
from jax.sharding import PartitionSpec as P

SIDE = 32
LANES = 128
step_size = 0.25


def to_bands(tiles):
    group = lax.broadcasted_iota(jnp.int32, tiles[0].shape, 1) // SIDE
    bands = []
    for band in range(8):
        out = None
        for slot in range(4):
            turn = SIDE * ((slot - band) % 4)
            tile = tiles[2 * slot + band // 4]
            tile = pltpu.roll(tile, turn, 1) if turn else tile
            out = tile if out is None else jnp.where(group == slot, tile, out)
        bands.append(out)
    return bands


def from_bands(bands):
    group = lax.broadcasted_iota(jnp.int32, bands[0].shape, 1) // SIDE
    tiles = []
    for tile in range(8):
        out = None
        for slot in range(4):
            turn = SIDE * ((slot - tile // 2) % 4)
            band = bands[4 * (tile % 2) + slot]
            band = pltpu.roll(band, turn, 1) if turn else band
            out = band if out is None else jnp.where(group == slot, band, out)
        tiles.append(out)
    return tiles


def split_lanes(value):
    return [value[:, LANES * k : LANES * (k + 1)] for k in range(value.shape[1] // LANES)]


def conv_layers(state_ref, weight_ref, bias_ref, first, last, unroll):
    ch = state_ref.shape[1]
    lane = lax.broadcasted_iota(jnp.int32, (ch, LANES), 1)
    column = lane % SIDE
    not_first, not_last = column != 0, column != SIDE - 1
    below, above = lane >= SIDE, lane < LANES - SIDE

    def layer(index, unused):
        weight = weight_ref[index]
        rows = jnp.concatenate([weight[:, 3 * ch * k : 3 * ch * (k + 1)] for k in range(3)], axis=0)
        bias = bias_ref[index]
        left, mid, right = [], [], []
        for band in range(8):
            value = state_ref[band]
            value = value.astype(jnp.bfloat16)
            zero = jnp.zeros_like(value)
            left.append(jnp.where(not_first, pltpu.roll(value, 1, 1), zero))
            mid.append(value)
            right.append(jnp.where(not_last, pltpu.roll(value, LANES - 1, 1), zero))
        taps = []
        for pair in range(4):
            stack = jnp.concatenate(
                [jnp.concatenate(part[2 * pair : 2 * pair + 2], axis=1) for part in (left, mid, right)], axis=0
            )
            full = jnp.dot(rows, stack, preferred_element_type=jnp.float32)
            taps += [full[:, :LANES], full[:, LANES:]]
        for band in range(8):
            up = taps[band - 1][:ch]
            if band == 0:
                up = jnp.where(below, pltpu.roll(up, SIDE, 1), 0.0)
            down = taps[(band + 1) % 8][2 * ch :]
            if band == 7:
                down = jnp.where(above, pltpu.roll(down, LANES - SIDE, 1), 0.0)
            mixed = taps[band][ch : 2 * ch] + up + down
            state_ref[band] = state_ref[band] + step_size * jnp.tanh(mixed + bias)
        return unused

    lax.fori_loop(first, last, layer, 0, unroll=unroll)


def split_float(value):
    coarse = value.astype(jnp.bfloat16)
    return coarse, (value - coarse.astype(jnp.float32)).astype(jnp.bfloat16)


def cycle_kernel(
    count,
    start_ref,
    input_ref,
    weight_hbm,
    bias_ref,
    matrix_ref,
    change_ref,
    correction_ref,
    weights,
    biases,
    state,
    origin,
    starts_out,
    ends_out,
    input_out,
    matrices,
    coarse_high,
    coarse_low,
    starts,
    ends,
    chain,
    returned,
    load_sems,
    send_sems,
    recv_sems,
):
    me = lax.axis_index("layer")
    core = lax.rem(me, 2)
    chips = count // 2
    ch, pixels = start_ref.shape
    layers = weights.shape[0]
    share = pixels // 2 // count
    early, late = layers // 6, 2 * layers // 3
    unroll = 4 if early % 4 == 0 else 1

    loads = [
        pltpu.make_async_copy(weight_hbm.at[part], weights.at[part], load_sems.at[number])
        for number, part in enumerate((pl.ds(0, early), pl.ds(early, layers - early)))
    ]
    for load in loads:
        load.start()

    def slice_of(owner):
        return pl.ds(pl.multiple_of(owner * share, share), share)

    def push(source, target, number, peer):
        return pltpu.make_async_remote_copy(
            src_ref=source,
            dst_ref=target,
            send_sem=send_sems.at[number],
            recv_sem=recv_sems.at[number],
            device_id={"layer": peer},
            device_id_type=pl.DeviceIdType.MESH,
        )

    def peers(action, stride=1):
        def turn(offset, unused):
            action(lax.rem(me + offset * stride, count))
            return unused

        lax.fori_loop(1, count // stride, turn, 0, unroll=3 if stride == 1 else 1)

    def all_of(buffer, number):
        return push(buffer, buffer, number, lax.rem(me + 1, count))

    def packed(bands):
        return [jnp.concatenate([bands[k], bands[k + 4]], axis=0).T for k in range(4)]

    barrier = pltpu.get_barrier_semaphore()
    peers(
        lambda peer: pl.semaphore_signal(
            barrier, inc=1, device_id={"layer": peer}, device_id_type=pl.DeviceIdType.MESH
        )
    )
    turned = matrix_ref[...].T
    matrices[core, me // 2] = jnp.concatenate([turned[: ch // 2], turned[ch // 2 :]], axis=1)
    columns = bias_ref[...].T
    for index in range(layers):
        biases[index] = jnp.broadcast_to(columns[:, index : index + 1], (ch, LANES))
    bands = to_bands(split_lanes(start_ref[...]))
    for band in range(8):
        state[band] = bands[band]
        origin[band] = bands[band]
    for part, value in enumerate(packed(bands)):
        starts_out[LANES * part : LANES * (part + 1), :] = value
    starts[me] = starts_out[slice_of(me), :]
    loads[0].wait()
    conv_layers(state, weights, biases, 0, early, unroll)

    pl.semaphore_wait(barrier, count - 1)
    own = matrices.at[core, me // 2]
    peers(lambda peer: push(own, own, 0, peer).start(), 2)
    peers(lambda peer: push(starts_out.at[slice_of(peer)], starts.at[me], 1, peer).start())
    loads[1].wait()
    conv_layers(state, weights, biases, early, late, unroll)

    all_of(matrices.at[0, pl.ds(0, chips - 1)], 0).wait_recv()
    across = push(matrices.at[core], matrices.at[core], 4, me + 1 - 2 * core)
    across.start()
    conv_layers(state, weights, biases, late, layers, unroll)

    for part, value in enumerate(packed([state[band] for band in range(8)])):
        ends_out[LANES * part : LANES * (part + 1), :] = value
    ends[me] = ends_out[slice_of(me), :]
    peers(lambda peer: push(ends_out.at[slice_of(peer)], ends.at[me], 2, peer).start())
    for part, value in enumerate(packed(to_bands(split_lanes(input_ref[...])))):
        input_out[LANES * part : LANES * (part + 1), :] = value
    across.wait_recv()
    lower = lax.broadcasted_iota(jnp.int32, (ch // 2, LANES), 1) < ch

    def widen(index, unused):
        pair = matrices[lax.rem(index, 2), index // 2]
        swapped = pltpu.roll(pair, ch, 1)
        wide = jnp.concatenate(
            [
                jnp.where(lower, pair, 0.0),
                jnp.where(lower, swapped, 0.0),
                jnp.where(lower, 0.0, swapped),
                jnp.where(lower, 0.0, pair),
            ],
            axis=0,
        )
        high, low = split_float(wide)
        coarse_high[index] = high
        coarse_low[index] = low
        return unused

    lax.fori_loop(0, count - 1, widen, 0, unroll=3)
    all_of(starts.at[pl.ds(0, count - 1)], 1).wait_recv()
    all_of(ends.at[pl.ds(0, count - 1)], 2).wait_recv()

    def give(index):
        @pl.when(index != me)
        def _():
            push(chain.at[index], returned.at[me], 3, index).start()

    def chain_step(index, current):
        matrix_high, matrix_low = coarse_high[index - 1], coarse_low[index - 1]
        high, low = split_float(current)
        both = jnp.dot(
            jnp.concatenate([high, low], axis=0), matrix_high, preferred_element_type=jnp.float32
        )
        rest = jnp.dot(high, matrix_low, preferred_element_type=jnp.float32)
        current = both[:share] + both[share:] + rest + (ends[index - 1] - starts[index])
        chain[index] = current
        give(index - 1)
        return current

    first = input_out[slice_of(me), :] - starts[0]
    chain[0] = first
    lax.fori_loop(1, count, chain_step, first, unroll=3)
    give(count - 1)
    returned[me] = chain[me]
    all_of(returned.at[pl.ds(0, count - 1)], 3).wait_recv()

    gathered = returned[...].reshape(pixels // 2, LANES)
    correction = [None] * 8
    for part in range(4):
        both = gathered[LANES * part : LANES * (part + 1)].T
        correction[part] = both[:ch]
        correction[part + 4] = both[ch:]
    for band in range(8):
        state[band] = origin[band] + correction[band]
        origin[band] = state[band]
    for tile, value in enumerate(from_bands(correction)):
        correction_ref[:, LANES * tile : LANES * (tile + 1)] = value
    conv_layers(state, weights, biases, 0, layers, unroll)
    for tile, value in enumerate(from_bands([state[band] - origin[band] for band in range(8)])):
        change_ref[:, LANES * tile : LANES * (tile + 1)] = value
    all_of(matrices.at[0, pl.ds(0, chips - 1)], 0).wait_send()
    across.wait_send()
    for number, buffer in ((1, starts), (2, ends), (3, returned)):
        all_of(buffer.at[pl.ds(0, count - 1)], number).wait_send()


def on_device(cpoints, network_input, conv_weight, conv_bias, coarse_matrix):
    ch, pixels = network_input.shape[1:]
    layers = conv_bias.shape[0]
    count = lax.axis_size("layer")
    share = pixels // 2 // count
    state = jax.ShapeDtypeStruct((ch, pixels), jnp.float32)
    banded = pltpu.VMEM((8, ch, LANES), jnp.float32)
    sent = pltpu.VMEM((pixels // 2, LANES), jnp.float32)
    gathered = pltpu.VMEM((count, share, LANES), jnp.float32)
    wide = pltpu.VMEM((count, LANES, LANES), jnp.bfloat16)
    vmem = pl.BlockSpec(memory_space=pltpu.VMEM)
    change, correction = pl.pallas_call(
        functools.partial(cycle_kernel, count),
        out_shape=(state, state),
        in_specs=[vmem, vmem, pl.BlockSpec(memory_space=pl.ANY), vmem, vmem],
        out_specs=(vmem, vmem),
        scratch_shapes=[
            pltpu.VMEM(conv_weight.shape, conv_weight.dtype),
            pltpu.VMEM((layers, ch, LANES), jnp.float32),
            banded,
            banded,
            sent,
            sent,
            sent,
            pltpu.VMEM((2, count // 2, ch // 2, LANES), jnp.float32),
            wide,
            wide,
            gathered,
            gathered,
            gathered,
            gathered,
            pltpu.SemaphoreType.DMA((2,)),
            pltpu.SemaphoreType.DMA((5,)),
            pltpu.SemaphoreType.DMA((5,)),
        ],
        compiler_params=pltpu.CompilerParams(
            collective_id=0, has_side_effects=True, vmem_limit_bytes=60 << 20
        ),
    )(cpoints[0, 0], network_input[0], conv_weight, conv_bias, coarse_matrix[0])
    corrected = cpoints[0, 0] + correction
    return ((corrected + change)[None, None], corrected[None, None])


def solution(mesh):
    placed = (
        P("layer", "dp", None, None),
        P("dp", None, None),
        P("layer", None, None),
        P("layer", None),
        P("layer", None, None),
    )
    return jax.shard_map(
        on_device,
        mesh=mesh,
        in_specs=placed,
        out_specs=(P("layer", "dp", None, None), P("layer", "dp", None, None)),
        check_vma=False,
    )
```

```python
import functools
import jax
import jax.numpy as jnp
from jax import lax
from jax.experimental import pallas as pl
from jax.experimental.pallas import tpu as pltpu
from jax.sharding import PartitionSpec as P

SIDE = 32
LANES = 128
step_size = 0.25


def to_bands(tiles):
    group = lax.broadcasted_iota(jnp.int32, tiles[0].shape, 1) // SIDE
    bands = []
    for band in range(8):
        out = None
        for slot in range(4):
            turn = SIDE * ((slot - band) % 4)
            tile = tiles[2 * slot + band // 4]
            tile = pltpu.roll(tile, turn, 1) if turn else tile
            out = tile if out is None else jnp.where(group == slot, tile, out)
        bands.append(out)
    return bands


def from_bands(bands):
    group = lax.broadcasted_iota(jnp.int32, bands[0].shape, 1) // SIDE
    tiles = []
    for tile in range(8):
        out = None
        for slot in range(4):
            turn = SIDE * ((slot - tile // 2) % 4)
            band = bands[4 * (tile % 2) + slot]
            band = pltpu.roll(band, turn, 1) if turn else band
            out = band if out is None else jnp.where(group == slot, band, out)
        tiles.append(out)
    return tiles


def split_lanes(value):
    return [value[:, LANES * k : LANES * (k + 1)] for k in range(value.shape[1] // LANES)]


def conv_layers(state_ref, weight_ref, rows_ref, bias_ref, first, last, unroll, fresh):
    ch = state_ref.shape[1]
    lane = lax.broadcasted_iota(jnp.int32, (ch, LANES), 1)
    column = lane % SIDE
    not_first, not_last = column != 0, column != SIDE - 1
    below, above = lane >= SIDE, lane < LANES - SIDE

    def layer(index, unused):
        if fresh:
            weight = weight_ref[index]
            rows = jnp.concatenate([weight[:, 3 * ch * k : 3 * ch * (k + 1)] for k in range(3)], axis=0)
            rows_ref[index] = rows
        else:
            rows = rows_ref[index]
        bias = bias_ref[index]
        left, mid, right = [], [], []
        for band in range(8):
            value = state_ref[band]
            value = value.astype(jnp.bfloat16)
            zero = jnp.zeros_like(value)
            left.append(jnp.where(not_first, pltpu.roll(value, 1, 1), zero))
            mid.append(value)
            right.append(jnp.where(not_last, pltpu.roll(value, LANES - 1, 1), zero))
        taps = []
        for pair in range(4):
            stack = jnp.concatenate(
                [jnp.concatenate(part[2 * pair : 2 * pair + 2], axis=1) for part in (left, mid, right)], axis=0
            )
            full = jnp.dot(rows, stack, preferred_element_type=jnp.float32)
            taps += [full[:, :LANES], full[:, LANES:]]
        for band in range(8):
            up = taps[band - 1][:ch]
            if band == 0:
                up = jnp.where(below, pltpu.roll(up, SIDE, 1), 0.0)
            down = taps[(band + 1) % 8][2 * ch :]
            if band == 7:
                down = jnp.where(above, pltpu.roll(down, LANES - SIDE, 1), 0.0)
            mixed = taps[band][ch : 2 * ch] + up + down
            state_ref[band] = state_ref[band] + step_size * jnp.tanh(mixed + bias)
        return unused

    lax.fori_loop(first, last, layer, 0, unroll=unroll)


def split_float(value):
    coarse = value.astype(jnp.bfloat16)
    return coarse, (value - coarse.astype(jnp.float32)).astype(jnp.bfloat16)


def cycle_kernel(
    count,
    start_ref,
    input_ref,
    weight_hbm,
    bias_ref,
    matrix_ref,
    change_ref,
    correction_ref,
    weights,
    stacked,
    biases,
    state,
    origin,
    starts_out,
    ends_out,
    input_out,
    matrices,
    coarse_high,
    coarse_low,
    starts,
    ends,
    chain,
    returned,
    load_sems,
    send_sems,
    recv_sems,
):
    me = lax.axis_index("layer")
    core = lax.rem(me, 2)
    chips = count // 2
    ch, pixels = start_ref.shape
    layers = weights.shape[0]
    share = pixels // 2 // count
    early, late = layers // 6, 5 * layers // 6
    unroll = 4 if early % 4 == 0 else 1

    loads = [
        pltpu.make_async_copy(weight_hbm.at[part], weights.at[part], load_sems.at[number])
        for number, part in enumerate((pl.ds(0, early), pl.ds(early, layers - early)))
    ]
    for load in loads:
        load.start()

    def slice_of(owner):
        return pl.ds(pl.multiple_of(owner * share, share), share)

    def push(source, target, number, peer):
        return pltpu.make_async_remote_copy(
            src_ref=source,
            dst_ref=target,
            send_sem=send_sems.at[number],
            recv_sem=recv_sems.at[number],
            device_id={"layer": peer},
            device_id_type=pl.DeviceIdType.MESH,
        )

    def peers(action, stride=1):
        def turn(offset, unused):
            action(lax.rem(me + offset * stride, count))
            return unused

        lax.fori_loop(1, count // stride, turn, 0, unroll=3 if stride == 1 else 1)

    def all_of(buffer, number):
        return push(buffer, buffer, number, lax.rem(me + 1, count))

    def packed(bands):
        return [jnp.concatenate([bands[k], bands[k + 4]], axis=0).T for k in range(4)]

    barrier = pltpu.get_barrier_semaphore()
    peers(
        lambda peer: pl.semaphore_signal(
            barrier, inc=1, device_id={"layer": peer}, device_id_type=pl.DeviceIdType.MESH
        )
    )
    turned = matrix_ref[...].T
    matrices[core, me // 2] = jnp.concatenate([turned[: ch // 2], turned[ch // 2 :]], axis=1)
    columns = bias_ref[...].T
    for index in range(layers):
        biases[index] = jnp.broadcast_to(columns[:, index : index + 1], (ch, LANES))
    bands = to_bands(split_lanes(start_ref[...]))
    for band in range(8):
        state[band] = bands[band]
        origin[band] = bands[band]
    for part, value in enumerate(packed(bands)):
        starts_out[LANES * part : LANES * (part + 1), :] = value
    starts[me] = starts_out[slice_of(me), :]
    loads[0].wait()
    conv_layers(state, weights, stacked, biases, 0, early, unroll, True)

    pl.semaphore_wait(barrier, count - 1)
    own = matrices.at[core, me // 2]
    peers(lambda peer: push(own, own, 0, peer).start(), 2)
    peers(lambda peer: push(starts_out.at[slice_of(peer)], starts.at[me], 1, peer).start())
    loads[1].wait()
    conv_layers(state, weights, stacked, biases, early, late, unroll, True)

    all_of(matrices.at[0, pl.ds(0, chips - 1)], 0).wait_recv()
    across = push(matrices.at[core], matrices.at[core], 4, me + 1 - 2 * core)
    across.start()
    conv_layers(state, weights, stacked, biases, late, layers, unroll, True)

    for part, value in enumerate(packed([state[band] for band in range(8)])):
        ends_out[LANES * part : LANES * (part + 1), :] = value
    ends[me] = ends_out[slice_of(me), :]
    peers(lambda peer: push(ends_out.at[slice_of(peer)], ends.at[me], 2, peer).start())
    for part, value in enumerate(packed(to_bands(split_lanes(input_ref[...])))):
        input_out[LANES * part : LANES * (part + 1), :] = value
    across.wait_recv()
    lower = lax.broadcasted_iota(jnp.int32, (ch // 2, LANES), 1) < ch

    def widen(index, unused):
        pair = matrices[lax.rem(index, 2), index // 2]
        swapped = pltpu.roll(pair, ch, 1)
        wide = jnp.concatenate(
            [
                jnp.where(lower, pair, 0.0),
                jnp.where(lower, swapped, 0.0),
                jnp.where(lower, 0.0, swapped),
                jnp.where(lower, 0.0, pair),
            ],
            axis=0,
        )
        high, low = split_float(wide)
        coarse_high[index] = high
        coarse_low[index] = low
        return unused

    lax.fori_loop(0, count - 1, widen, 0, unroll=3)
    all_of(starts.at[pl.ds(0, count - 1)], 1).wait_recv()
    all_of(ends.at[pl.ds(0, count - 1)], 2).wait_recv()

    def give(index):
        @pl.when(index != me)
        def _():
            push(chain.at[index], returned.at[me], 3, index).start()

    def chain_step(index, current):
        matrix_high, matrix_low = coarse_high[index - 1], coarse_low[index - 1]
        high, low = split_float(current)
        both = jnp.dot(
            jnp.concatenate([high, low], axis=0), matrix_high, preferred_element_type=jnp.float32
        )
        rest = jnp.dot(high, matrix_low, preferred_element_type=jnp.float32)
        current = both[:share] + both[share:] + rest + (ends[index - 1] - starts[index])
        chain[index] = current
        give(index - 1)
        return current

    first = input_out[slice_of(me), :] - starts[0]
    chain[0] = first
    lax.fori_loop(1, count, chain_step, first, unroll=3)
    give(count - 1)
    returned[me] = chain[me]
    all_of(returned.at[pl.ds(0, count - 1)], 3).wait_recv()

    gathered = returned[...].reshape(pixels // 2, LANES)
    correction = [None] * 8
    for part in range(4):
        both = gathered[LANES * part : LANES * (part + 1)].T
        correction[part] = both[:ch]
        correction[part + 4] = both[ch:]
    for band in range(8):
        state[band] = origin[band] + correction[band]
        origin[band] = state[band]
    for tile, value in enumerate(from_bands(correction)):
        correction_ref[:, LANES * tile : LANES * (tile + 1)] = value
    conv_layers(state, weights, stacked, biases, 0, layers, unroll, False)
    for tile, value in enumerate(from_bands([state[band] - origin[band] for band in range(8)])):
        change_ref[:, LANES * tile : LANES * (tile + 1)] = value
    all_of(matrices.at[0, pl.ds(0, chips - 1)], 0).wait_send()
    across.wait_send()
    for number, buffer in ((1, starts), (2, ends), (3, returned)):
        all_of(buffer.at[pl.ds(0, count - 1)], number).wait_send()


def on_device(cpoints, network_input, conv_weight, conv_bias, coarse_matrix):
    ch, pixels = network_input.shape[1:]
    layers = conv_bias.shape[0]
    count = lax.axis_size("layer")
    share = pixels // 2 // count
    state = jax.ShapeDtypeStruct((ch, pixels), jnp.float32)
    banded = pltpu.VMEM((8, ch, LANES), jnp.float32)
    sent = pltpu.VMEM((pixels // 2, LANES), jnp.float32)
    gathered = pltpu.VMEM((count, share, LANES), jnp.float32)
    wide = pltpu.VMEM((count, LANES, LANES), jnp.bfloat16)
    vmem = pl.BlockSpec(memory_space=pltpu.VMEM)
    change, correction = pl.pallas_call(
        functools.partial(cycle_kernel, count),
        out_shape=(state, state),
        in_specs=[vmem, vmem, pl.BlockSpec(memory_space=pl.ANY), vmem, vmem],
        out_specs=(vmem, vmem),
        scratch_shapes=[
            pltpu.VMEM(conv_weight.shape, conv_weight.dtype),
            pltpu.VMEM((layers, 3 * ch, 3 * ch), conv_weight.dtype),
            pltpu.VMEM((layers, ch, LANES), jnp.float32),
            banded,
            banded,
            sent,
            sent,
            sent,
            pltpu.VMEM((2, count // 2, ch // 2, LANES), jnp.float32),
            wide,
            wide,
            gathered,
            gathered,
            gathered,
            gathered,
            pltpu.SemaphoreType.DMA((2,)),
            pltpu.SemaphoreType.DMA((5,)),
            pltpu.SemaphoreType.DMA((5,)),
        ],
        compiler_params=pltpu.CompilerParams(
            collective_id=0, has_side_effects=True, vmem_limit_bytes=60 << 20
        ),
    )(cpoints[0, 0], network_input[0], conv_weight, conv_bias, coarse_matrix[0])
    corrected = cpoints[0, 0] + correction
    return ((corrected + change)[None, None], corrected[None, None])


def solution(mesh):
    placed = (
        P("layer", "dp", None, None),
        P("dp", None, None),
        P("layer", None, None),
        P("layer", None),
        P("layer", None, None),
    )
    return jax.shard_map(
        on_device,
        mesh=mesh,
        in_specs=placed,
        out_specs=(P("layer", "dp", None, None), P("layer", "dp", None, None)),
        check_vma=False,
    )
```

```python
import functools
import jax
import jax.numpy as jnp
from jax import lax
from jax.experimental import pallas as pl
from jax.experimental.pallas import tpu as pltpu
from jax.sharding import PartitionSpec as P

SIDE = 32
LANES = 128
step_size = 0.25


def to_bands(tiles):
    group = lax.broadcasted_iota(jnp.int32, tiles[0].shape, 1) // SIDE
    bands = []
    for band in range(8):
        out = None
        for slot in range(4):
            turn = SIDE * ((slot - band) % 4)
            tile = tiles[2 * slot + band // 4]
            tile = pltpu.roll(tile, turn, 1) if turn else tile
            out = tile if out is None else jnp.where(group == slot, tile, out)
        bands.append(out)
    return bands


def from_bands(bands):
    group = lax.broadcasted_iota(jnp.int32, bands[0].shape, 1) // SIDE
    tiles = []
    for tile in range(8):
        out = None
        for slot in range(4):
            turn = SIDE * ((slot - tile // 2) % 4)
            band = bands[4 * (tile % 2) + slot]
            band = pltpu.roll(band, turn, 1) if turn else band
            out = band if out is None else jnp.where(group == slot, band, out)
        tiles.append(out)
    return tiles


def split_lanes(value):
    return [value[:, LANES * k : LANES * (k + 1)] for k in range(value.shape[1] // LANES)]


def conv_layers(state_ref, weight_ref, rows_ref, bias_ref, first, last, unroll, fresh):
    ch = state_ref.shape[1]
    lane = lax.broadcasted_iota(jnp.int32, (ch, LANES), 1)
    column = lane % SIDE
    not_first, not_last = column != 0, column != SIDE - 1
    below, above = lane >= SIDE, lane < LANES - SIDE

    def layer(index, unused):
        if fresh:
            weight = weight_ref[index]
            rows = jnp.concatenate([weight[:, 3 * ch * k : 3 * ch * (k + 1)] for k in range(3)], axis=0)
            rows_ref[index] = rows
        else:
            rows = rows_ref[index]
        bias = bias_ref[index]
        left, mid, right = [], [], []
        for band in range(8):
            value = state_ref[band]
            value = value.astype(jnp.bfloat16)
            zero = jnp.zeros_like(value)
            left.append(jnp.where(not_first, pltpu.roll(value, 1, 1), zero))
            mid.append(value)
            right.append(jnp.where(not_last, pltpu.roll(value, LANES - 1, 1), zero))
        taps = []
        for pair in range(4):
            stack = jnp.concatenate(
                [jnp.concatenate(part[2 * pair : 2 * pair + 2], axis=1) for part in (left, mid, right)], axis=0
            )
            full = jnp.dot(rows, stack, preferred_element_type=jnp.float32)
            taps += [full[:, :LANES], full[:, LANES:]]
        for band in range(8):
            up = taps[band - 1][:ch]
            if band == 0:
                up = jnp.where(below, pltpu.roll(up, SIDE, 1), 0.0)
            down = taps[(band + 1) % 8][2 * ch :]
            if band == 7:
                down = jnp.where(above, pltpu.roll(down, LANES - SIDE, 1), 0.0)
            mixed = taps[band][ch : 2 * ch] + up + down
            state_ref[band] = state_ref[band] + step_size * jnp.tanh(mixed + bias)
        return unused

    lax.fori_loop(first, last, layer, 0, unroll=unroll)


def split_float(value):
    coarse = value.astype(jnp.bfloat16)
    return coarse, (value - coarse.astype(jnp.float32)).astype(jnp.bfloat16)


def cycle_kernel(
    count,
    start_ref,
    input_ref,
    weight_hbm,
    bias_ref,
    matrix_ref,
    change_ref,
    correction_ref,
    weights,
    stacked,
    biases,
    state,
    origin,
    starts_out,
    ends_out,
    input_out,
    matrices,
    coarse_high,
    coarse_low,
    starts,
    ends,
    chain,
    returned,
    load_sems,
    send_sems,
    recv_sems,
):
    me = lax.axis_index("layer")
    core = lax.rem(me, 2)
    crowd = min(8, count)
    chips = count // 2
    ch, pixels = start_ref.shape
    layers = weights.shape[0]
    share = pixels // 2 // count
    early, late = layers // 6, 5 * layers // 6
    unroll = 4 if early % 4 == 0 else 1

    loads = [
        pltpu.make_async_copy(weight_hbm.at[part], weights.at[part], load_sems.at[number])
        for number, part in enumerate((pl.ds(0, early), pl.ds(early, layers - early)))
    ]
    for load in loads:
        load.start()

    def slice_of(owner):
        return pl.ds(pl.multiple_of(owner * share, share), share)

    def push(source, target, number, peer, arrival=None):
        return pltpu.make_async_remote_copy(
            src_ref=source,
            dst_ref=target,
            send_sem=send_sems.at[number],
            recv_sem=recv_sems.at[number if arrival is None else arrival],
            device_id={"layer": peer},
            device_id_type=pl.DeviceIdType.MESH,
        )

    def peers(action, stride=1):
        def turn(offset, unused):
            action(lax.rem(me + offset * stride, count))
            return unused

        lax.fori_loop(1, count // stride, turn, 0, unroll=3 if stride == 1 else 1)

    def all_of(buffer, number):
        return push(buffer, buffer, number, lax.rem(me + 1, count))

    def packed(bands):
        return [jnp.concatenate([bands[k], bands[k + 4]], axis=0).T for k in range(4)]

    barrier = pltpu.get_barrier_semaphore()
    peers(
        lambda peer: pl.semaphore_signal(
            barrier, inc=1, device_id={"layer": peer}, device_id_type=pl.DeviceIdType.MESH
        )
    )
    turned = matrix_ref[...].T
    matrices[core, me // 2] = jnp.concatenate([turned[: ch // 2], turned[ch // 2 :]], axis=1)
    columns = bias_ref[...].T
    for index in range(layers):
        biases[index] = jnp.broadcast_to(columns[:, index : index + 1], (ch, LANES))
    bands = to_bands(split_lanes(start_ref[...]))
    for band in range(8):
        state[band] = bands[band]
        origin[band] = bands[band]
    for part, value in enumerate(packed(bands)):
        starts_out[LANES * part : LANES * (part + 1), :] = value
    starts[me] = starts_out[slice_of(me), :]
    loads[0].wait()
    conv_layers(state, weights, stacked, biases, 0, early, unroll, True)

    pl.semaphore_wait(barrier, count - 1)
    own = matrices.at[core, me // 2]
    peers(lambda peer: push(own, own, 0, peer).start(), 2)
    peers(lambda peer: push(starts_out.at[slice_of(peer)], starts.at[me], 1, peer).start())
    loads[1].wait()
    conv_layers(state, weights, stacked, biases, early, late, unroll, True)

    all_of(matrices.at[0, pl.ds(0, chips - 1)], 0).wait_recv()
    across = push(matrices.at[core], matrices.at[core], 4, me + 1 - 2 * core)
    across.start()
    conv_layers(state, weights, stacked, biases, late, layers, unroll, True)

    for part, value in enumerate(packed([state[band] for band in range(8)])):
        ends_out[LANES * part : LANES * (part + 1), :] = value
    arrival = 5 + me // crowd
    peers(lambda peer: push(ends_out.at[slice_of(peer)], ends.at[me], 2, peer, arrival).start())
    pltpu.make_async_copy(ends_out.at[slice_of(me)], ends.at[me], recv_sems.at[arrival]).start()
    for part, value in enumerate(packed(to_bands(split_lanes(input_ref[...])))):
        input_out[LANES * part : LANES * (part + 1), :] = value
    across.wait_recv()
    lower = lax.broadcasted_iota(jnp.int32, (ch // 2, LANES), 1) < ch

    def widen(index, unused):
        pair = matrices[lax.rem(index, 2), index // 2]
        swapped = pltpu.roll(pair, ch, 1)
        wide = jnp.concatenate(
            [
                jnp.where(lower, pair, 0.0),
                jnp.where(lower, swapped, 0.0),
                jnp.where(lower, 0.0, swapped),
                jnp.where(lower, 0.0, pair),
            ],
            axis=0,
        )
        high, low = split_float(wide)
        coarse_high[index] = high
        coarse_low[index] = low
        return unused

    lax.fori_loop(0, count - 1, widen, 0, unroll=3)
    all_of(starts.at[pl.ds(0, count - 1)], 1).wait_recv()

    def give(index):
        @pl.when(index != me)
        def _():
            push(chain.at[index], returned.at[me], 3, index).start()

    def chain_step(index, current):
        matrix_high, matrix_low = coarse_high[index - 1], coarse_low[index - 1]
        high, low = split_float(current)
        both = jnp.dot(
            jnp.concatenate([high, low], axis=0), matrix_high, preferred_element_type=jnp.float32
        )
        rest = jnp.dot(high, matrix_low, preferred_element_type=jnp.float32)
        current = both[:share] + both[share:] + rest + (ends[index - 1] - starts[index])
        chain[index] = current
        give(index - 1)
        return current

    first = input_out[slice_of(me), :] - starts[0]
    chain[0] = first

    def crowd_steps(group, current, steps):
        part = ends.at[pl.ds(group * crowd, crowd)]
        push(part, part, 2, lax.rem(me + 1, count), 5 + group).wait_recv()
        for step in range(1, steps + 1):
            current = chain_step(group * crowd + step, current)
        return current

    groups = count // crowd
    current = lax.fori_loop(0, groups - 1, lambda group, value: crowd_steps(group, value, crowd), first)
    crowd_steps(groups - 1, current, crowd - 1)
    give(count - 1)
    returned[me] = chain[me]
    all_of(returned.at[pl.ds(0, count - 1)], 3).wait_recv()

    gathered = returned[...].reshape(pixels // 2, LANES)
    correction = [None] * 8
    for part in range(4):
        both = gathered[LANES * part : LANES * (part + 1)].T
        correction[part] = both[:ch]
        correction[part + 4] = both[ch:]
    for band in range(8):
        state[band] = origin[band] + correction[band]
        origin[band] = state[band]
    for tile, value in enumerate(from_bands(correction)):
        correction_ref[:, LANES * tile : LANES * (tile + 1)] = value
    conv_layers(state, weights, stacked, biases, 0, layers, unroll, False)
    for tile, value in enumerate(from_bands([state[band] - origin[band] for band in range(8)])):
        change_ref[:, LANES * tile : LANES * (tile + 1)] = value
    all_of(matrices.at[0, pl.ds(0, chips - 1)], 0).wait_send()
    across.wait_send()
    for number, buffer in ((1, starts), (2, ends), (3, returned)):
        all_of(buffer.at[pl.ds(0, count - 1)], number).wait_send()


def on_device(cpoints, network_input, conv_weight, conv_bias, coarse_matrix):
    ch, pixels = network_input.shape[1:]
    layers = conv_bias.shape[0]
    count = lax.axis_size("layer")
    share = pixels // 2 // count
    state = jax.ShapeDtypeStruct((ch, pixels), jnp.float32)
    banded = pltpu.VMEM((8, ch, LANES), jnp.float32)
    sent = pltpu.VMEM((pixels // 2, LANES), jnp.float32)
    gathered = pltpu.VMEM((count, share, LANES), jnp.float32)
    wide = pltpu.VMEM((count, LANES, LANES), jnp.bfloat16)
    vmem = pl.BlockSpec(memory_space=pltpu.VMEM)
    change, correction = pl.pallas_call(
        functools.partial(cycle_kernel, count),
        out_shape=(state, state),
        in_specs=[vmem, vmem, pl.BlockSpec(memory_space=pl.ANY), vmem, vmem],
        out_specs=(vmem, vmem),
        scratch_shapes=[
            pltpu.VMEM(conv_weight.shape, conv_weight.dtype),
            pltpu.VMEM((layers, 3 * ch, 3 * ch), conv_weight.dtype),
            pltpu.VMEM((layers, ch, LANES), jnp.float32),
            banded,
            banded,
            sent,
            sent,
            sent,
            pltpu.VMEM((2, count // 2, ch // 2, LANES), jnp.float32),
            wide,
            wide,
            gathered,
            gathered,
            gathered,
            gathered,
            pltpu.SemaphoreType.DMA((2,)),
            pltpu.SemaphoreType.DMA((5,)),
            pltpu.SemaphoreType.DMA((5 + count // min(8, count),)),
        ],
        compiler_params=pltpu.CompilerParams(
            collective_id=0, has_side_effects=True, vmem_limit_bytes=60 << 20
        ),
    )(cpoints[0, 0], network_input[0], conv_weight, conv_bias, coarse_matrix[0])
    corrected = cpoints[0, 0] + correction
    return ((corrected + change)[None, None], corrected[None, None])


def solution(mesh):
    placed = (
        P("layer", "dp", None, None),
        P("dp", None, None),
        P("layer", None, None),
        P("layer", None),
        P("layer", None, None),
    )
    return jax.shard_map(
        on_device,
        mesh=mesh,
        in_specs=placed,
        out_specs=(P("layer", "dp", None, None), P("layer", "dp", None, None)),
        check_vma=False,
    )
```

```python
import functools
import jax
import jax.numpy as jnp
from jax import lax
from jax.experimental import pallas as pl
from jax.experimental.pallas import tpu as pltpu
from jax.sharding import PartitionSpec as P

SIDE = 32
LANES = 128
step_size = 0.25


def to_bands(tiles):
    group = lax.broadcasted_iota(jnp.int32, tiles[0].shape, 1) // SIDE
    bands = []
    for band in range(8):
        out = None
        for slot in range(4):
            turn = SIDE * ((slot - band) % 4)
            tile = tiles[2 * slot + band // 4]
            tile = pltpu.roll(tile, turn, 1) if turn else tile
            out = tile if out is None else jnp.where(group == slot, tile, out)
        bands.append(out)
    return bands


def from_bands(bands):
    group = lax.broadcasted_iota(jnp.int32, bands[0].shape, 1) // SIDE
    tiles = []
    for tile in range(8):
        out = None
        for slot in range(4):
            turn = SIDE * ((slot - tile // 2) % 4)
            band = bands[4 * (tile % 2) + slot]
            band = pltpu.roll(band, turn, 1) if turn else band
            out = band if out is None else jnp.where(group == slot, band, out)
        tiles.append(out)
    return tiles


def split_lanes(value):
    return [value[:, LANES * k : LANES * (k + 1)] for k in range(value.shape[1] // LANES)]


def conv_layers(state_ref, weight_ref, rows_ref, bias_ref, first, last, unroll, fresh):
    ch = state_ref.shape[1]
    lane = lax.broadcasted_iota(jnp.int32, (ch, LANES), 1)
    column = lane % SIDE
    not_first, not_last = column != 0, column != SIDE - 1
    below, above = lane >= SIDE, lane < LANES - SIDE

    def layer(index, unused):
        if fresh:
            weight = weight_ref[index]
            rows = jnp.concatenate([weight[:, 3 * ch * k : 3 * ch * (k + 1)] for k in range(3)], axis=0)
            rows_ref[index] = rows
        else:
            rows = rows_ref[index]
        bias = bias_ref[index]
        left, mid, right = [], [], []
        for band in range(8):
            value = state_ref[band]
            value = value.astype(jnp.bfloat16)
            zero = jnp.zeros_like(value)
            left.append(jnp.where(not_first, pltpu.roll(value, 1, 1), zero))
            mid.append(value)
            right.append(jnp.where(not_last, pltpu.roll(value, LANES - 1, 1), zero))
        taps = []
        for pair in range(4):
            stack = jnp.concatenate(
                [jnp.concatenate(part[2 * pair : 2 * pair + 2], axis=1) for part in (left, mid, right)], axis=0
            )
            full = jnp.dot(rows, stack, preferred_element_type=jnp.float32)
            taps += [full[:, :LANES], full[:, LANES:]]
        for band in range(8):
            up = taps[band - 1][:ch]
            if band == 0:
                up = jnp.where(below, pltpu.roll(up, SIDE, 1), 0.0)
            down = taps[(band + 1) % 8][2 * ch :]
            if band == 7:
                down = jnp.where(above, pltpu.roll(down, LANES - SIDE, 1), 0.0)
            mixed = taps[band][ch : 2 * ch] + up + down
            state_ref[band] = state_ref[band] + step_size * jnp.tanh(mixed + bias)
        return unused

    lax.fori_loop(first, last, layer, 0, unroll=unroll)


def split_float(value):
    coarse = value.astype(jnp.bfloat16)
    return coarse, (value - coarse.astype(jnp.float32)).astype(jnp.bfloat16)


def cycle_kernel(
    count,
    start_ref,
    input_ref,
    weight_hbm,
    bias_ref,
    matrix_ref,
    change_ref,
    correction_ref,
    weights,
    stacked,
    biases,
    state,
    origin,
    starts_out,
    ends_out,
    input_out,
    matrices,
    coarse_high,
    coarse_low,
    starts,
    ends,
    chain,
    returned,
    load_sems,
    send_sems,
    recv_sems,
):
    me = lax.axis_index("layer")
    core = lax.rem(me, 2)
    crowd = min(8, count)
    chips = count // 2
    ch, pixels = start_ref.shape
    layers = weights.shape[0]
    share = pixels // 2 // count
    early, late = layers // 6, 11 * layers // 12
    unroll = 4 if early % 4 == 0 else 1

    loads = [
        pltpu.make_async_copy(weight_hbm.at[part], weights.at[part], load_sems.at[number])
        for number, part in enumerate((pl.ds(0, early), pl.ds(early, layers - early)))
    ]
    for load in loads:
        load.start()

    def slice_of(owner):
        return pl.ds(pl.multiple_of(owner * share, share), share)

    def push(source, target, number, peer, arrival=None):
        return pltpu.make_async_remote_copy(
            src_ref=source,
            dst_ref=target,
            send_sem=send_sems.at[number],
            recv_sem=recv_sems.at[number if arrival is None else arrival],
            device_id={"layer": peer},
            device_id_type=pl.DeviceIdType.MESH,
        )

    def peers(action, stride=1):
        def turn(offset, unused):
            action(lax.rem(me + offset * stride, count))
            return unused

        lax.fori_loop(1, count // stride, turn, 0, unroll=3 if stride == 1 else 1)

    def all_of(buffer, number):
        return push(buffer, buffer, number, lax.rem(me + 1, count))

    def packed(bands):
        return [jnp.concatenate([bands[k], bands[k + 4]], axis=0).T for k in range(4)]

    barrier = pltpu.get_barrier_semaphore()
    peers(
        lambda peer: pl.semaphore_signal(
            barrier, inc=1, device_id={"layer": peer}, device_id_type=pl.DeviceIdType.MESH
        )
    )
    turned = matrix_ref[...].T
    matrices[core, me // 2] = jnp.concatenate([turned[: ch // 2], turned[ch // 2 :]], axis=1)
    columns = bias_ref[...].T
    for index in range(layers):
        biases[index] = jnp.broadcast_to(columns[:, index : index + 1], (ch, LANES))
    bands = to_bands(split_lanes(start_ref[...]))
    for band in range(8):
        state[band] = bands[band]
        origin[band] = bands[band]
    for part, value in enumerate(packed(bands)):
        starts_out[LANES * part : LANES * (part + 1), :] = value
    starts[me] = starts_out[slice_of(me), :]
    loads[0].wait()
    conv_layers(state, weights, stacked, biases, 0, early, unroll, True)

    pl.semaphore_wait(barrier, count - 1)
    own = matrices.at[core, me // 2]
    peers(lambda peer: push(own, own, 0, peer).start(), 2)
    peers(lambda peer: push(starts_out.at[slice_of(peer)], starts.at[me], 1, peer).start())
    loads[1].wait()
    conv_layers(state, weights, stacked, biases, early, late, unroll, True)

    all_of(matrices.at[0, pl.ds(0, chips - 1)], 0).wait_recv()
    across = push(matrices.at[core], matrices.at[core], 4, me + 1 - 2 * core)
    across.start()
    conv_layers(state, weights, stacked, biases, late, layers, unroll, True)

    for part, value in enumerate(packed([state[band] for band in range(8)])):
        ends_out[LANES * part : LANES * (part + 1), :] = value
    arrival = 5 + me // crowd
    peers(lambda peer: push(ends_out.at[slice_of(peer)], ends.at[me], 2, peer, arrival).start())
    pltpu.make_async_copy(ends_out.at[slice_of(me)], ends.at[me], recv_sems.at[arrival]).start()
    for part, value in enumerate(packed(to_bands(split_lanes(input_ref[...])))):
        input_out[LANES * part : LANES * (part + 1), :] = value
    across.wait_recv()
    lower = lax.broadcasted_iota(jnp.int32, (ch // 2, LANES), 1) < ch

    def widen(index, unused):
        pair = matrices[lax.rem(index, 2), index // 2]
        swapped = pltpu.roll(pair, ch, 1)
        wide = jnp.concatenate(
            [
                jnp.where(lower, pair, 0.0),
                jnp.where(lower, swapped, 0.0),
                jnp.where(lower, 0.0, swapped),
                jnp.where(lower, 0.0, pair),
            ],
            axis=0,
        )
        high, low = split_float(wide)
        coarse_high[index] = high
        coarse_low[index] = low
        return unused

    lax.fori_loop(0, count - 1, widen, 0, unroll=3)
    all_of(starts.at[pl.ds(0, count - 1)], 1).wait_recv()

    def give(index):
        @pl.when(index != me)
        def _():
            push(chain.at[index], returned.at[me], 3, index).start()

    def chain_step(index, current):
        matrix_high, matrix_low = coarse_high[index - 1], coarse_low[index - 1]
        high, low = split_float(current)
        both = jnp.dot(
            jnp.concatenate([high, low], axis=0), matrix_high, preferred_element_type=jnp.float32
        )
        rest = jnp.dot(high, matrix_low, preferred_element_type=jnp.float32)
        current = both[:share] + both[share:] + rest + (ends[index - 1] - starts[index])
        chain[index] = current
        give(index - 1)
        return current

    first = input_out[slice_of(me), :] - starts[0]
    chain[0] = first

    def crowd_steps(group, current, steps):
        part = ends.at[pl.ds(group * crowd, crowd)]
        push(part, part, 2, lax.rem(me + 1, count), 5 + group).wait_recv()
        for step in range(1, steps + 1):
            current = chain_step(group * crowd + step, current)
        return current

    groups = count // crowd
    current = lax.fori_loop(0, groups - 1, lambda group, value: crowd_steps(group, value, crowd), first)
    crowd_steps(groups - 1, current, crowd - 1)
    give(count - 1)
    returned[me] = chain[me]
    all_of(returned.at[pl.ds(0, count - 1)], 3).wait_recv()

    gathered = returned[...].reshape(pixels // 2, LANES)
    correction = [None] * 8
    for part in range(4):
        both = gathered[LANES * part : LANES * (part + 1)].T
        correction[part] = both[:ch]
        correction[part + 4] = both[ch:]
    for band in range(8):
        state[band] = origin[band] + correction[band]
        origin[band] = state[band]
    for tile, value in enumerate(from_bands(correction)):
        correction_ref[:, LANES * tile : LANES * (tile + 1)] = value
    conv_layers(state, weights, stacked, biases, 0, layers, unroll, False)
    for tile, value in enumerate(from_bands([state[band] - origin[band] for band in range(8)])):
        change_ref[:, LANES * tile : LANES * (tile + 1)] = value
    all_of(matrices.at[0, pl.ds(0, chips - 1)], 0).wait_send()
    across.wait_send()
    for number, buffer in ((1, starts), (2, ends), (3, returned)):
        all_of(buffer.at[pl.ds(0, count - 1)], number).wait_send()


def on_device(cpoints, network_input, conv_weight, conv_bias, coarse_matrix):
    ch, pixels = network_input.shape[1:]
    layers = conv_bias.shape[0]
    count = lax.axis_size("layer")
    share = pixels // 2 // count
    state = jax.ShapeDtypeStruct((ch, pixels), jnp.float32)
    banded = pltpu.VMEM((8, ch, LANES), jnp.float32)
    sent = pltpu.VMEM((pixels // 2, LANES), jnp.float32)
    gathered = pltpu.VMEM((count, share, LANES), jnp.float32)
    wide = pltpu.VMEM((count, LANES, LANES), jnp.bfloat16)
    vmem = pl.BlockSpec(memory_space=pltpu.VMEM)
    change, correction = pl.pallas_call(
        functools.partial(cycle_kernel, count),
        out_shape=(state, state),
        in_specs=[vmem, vmem, pl.BlockSpec(memory_space=pl.ANY), vmem, vmem],
        out_specs=(vmem, vmem),
        scratch_shapes=[
            pltpu.VMEM(conv_weight.shape, conv_weight.dtype),
            pltpu.VMEM((layers, 3 * ch, 3 * ch), conv_weight.dtype),
            pltpu.VMEM((layers, ch, LANES), jnp.float32),
            banded,
            banded,
            sent,
            sent,
            sent,
            pltpu.VMEM((2, count // 2, ch // 2, LANES), jnp.float32),
            wide,
            wide,
            gathered,
            gathered,
            gathered,
            gathered,
            pltpu.SemaphoreType.DMA((2,)),
            pltpu.SemaphoreType.DMA((5,)),
            pltpu.SemaphoreType.DMA((5 + count // min(8, count),)),
        ],
        compiler_params=pltpu.CompilerParams(
            collective_id=0, has_side_effects=True, vmem_limit_bytes=60 << 20
        ),
    )(cpoints[0, 0], network_input[0], conv_weight, conv_bias, coarse_matrix[0])
    corrected = cpoints[0, 0] + correction
    return ((corrected + change)[None, None], corrected[None, None])


def solution(mesh):
    placed = (
        P("layer", "dp", None, None),
        P("dp", None, None),
        P("layer", None, None),
        P("layer", None),
        P("layer", None, None),
    )
    return jax.shard_map(
        on_device,
        mesh=mesh,
        in_specs=placed,
        out_specs=(P("layer", "dp", None, None), P("layer", "dp", None, None)),
        check_vma=False,
    )
```
